512 devices in a mesh: param: 128 (over y, x_lo, z), ex: 4 (over x_hi, core).
Axes of the slice: x: 4 (x_hi: 2, x_lo: 2; x = x_hi * 2 + x_lo), y: 8, z: 8, core: 2. Of those that a mesh axis runs over, the one named last changes fastest.
Arguments:
- inputs: bfloat16 [4, 256, 8192], P('ex', 'param'), may hold values from -6 to 6
- cotangents: bfloat16 [4, 256, 16384], P('ex', None, 'param'), may hold values from -0.375 to 0.375
- sign_flips: bfloat16 [16384, 8192], P('param'), may hold values from -1 to 1, as said below
- sample_rows: int32 [8192], replicated, may hold values from 0 to 16383
- sample_columns: int32 [8192], replicated, may hold values from 0 to 8191
Outputs:
- sketch: float32 [4, 8192], P('ex', 'param')
The draws below stay inside these ranges and needn't reach their ends.
Inputs may be any that keep to these rules, and one draw needn't show every extreme that they name: `sign_flips`: every entry is +1 or -1.
All inputs are finite; a program needn't handle non-finite values.
Results may differ from the reference program's by a relative error of at most 0.0003.
Values may be sent and summed in bfloat16 or wider, within the bound.
No kernel may reach another device: no remote copies, remote signals or barrier semaphores. Data moves between devices by JAX's collectives and lax.ppermute only.
A program may use at most 64 MiB of HBM per device.

```python
import math
import jax
import jax.numpy as jnp
from jax import lax

D = 8192
F = 16384
TOK = 256
SAMPLES = 8192
EX = 4
N_PARAM = 128


def draw_sign_flips(key, part):
    coin_bits = jax.random.randint(key, (F, D), 0, 2)
    return (2 * coin_bits - 1).astype(jnp.float32).astype(jnp.bfloat16)


def set_ends(entries, rng, least, high):
    longest = entries.shape.index(max(entries.shape))
    spots = []
    for shift in (0, 1):
        where = [jax.random.randint(jax.random.fold_in(rng, axis), (), 0, length) for axis, length in enumerate(entries.shape)]
        where[longest] = (where[longest] + shift) % entries.shape[longest]
        spots.append(tuple(where))
    return entries.at[spots[0]].set(least).at[spots[1]].set(high)


def steps_of(stream_key, shape, cuts, smallest, high):
    gain = 1.0
    for dim, parts in cuts:
        heights = jax.random.uniform(jax.random.fold_in(jax.random.fold_in(stream_key, 6), dim), (parts,), jnp.float32, smallest / len(cuts), high / len(cuts))
        gain = gain * jnp.repeat(jnp.exp(heights), shape[dim] // parts).reshape((-1,) + (1,) * (len(shape) - 1 - dim))
    return gain


def scatter_about(stream_key, extent, width, limit, split=(), kind=jnp.bfloat16):
    array = width * jax.random.normal(stream_key, extent, jnp.float32)
    if split:
        array = array * steps_of(stream_key, extent, split, -0.22, 0.18)
    return jnp.clip(array, -limit, limit).astype(kind)


def setup_inputs(seed: int = 0) -> dict:
    seeds = jax.random.split(jax.random.key(seed), 6)
    return {
        "inputs": scatter_about(seeds[0], (EX, TOK, D), 1.0, 6.0, ((0, 4), (1, 128))),
        "cotangents": scatter_about(seeds[1], (EX, TOK, F), TOK ** -0.5, 0.375, ((0, 4), (2, 128))),
        "sign_flips": draw_sign_flips(jax.random.fold_in(seeds[5], 71), 0),
        "sample_rows": set_ends(jax.random.randint(seeds[3], (SAMPLES,), 0, F), jax.random.fold_in(seeds[3], 1), 0, F - 1).astype(jnp.int32),
        "sample_columns": set_ends(jax.random.randint(seeds[4], (SAMPLES,), 0, D), jax.random.fold_in(seeds[4], 1), 0, D - 1).astype(jnp.int32),
    }


def hadamard_table(order):
    positions = lax.iota(jnp.int32, order)
    shared = jnp.bitwise_and(positions[:, None], positions[None, :])
    parity = jnp.zeros((order, order), jnp.int32)
    for bit_place in range(order.bit_length() - 1):
        parity = parity + jnp.bitwise_and(jnp.right_shift(shared, bit_place), 1)
    parity = parity % 2
    return (1.0 - 2.0 * parity).astype(jnp.float32)

def walsh_transform(vector):
    length = vector.shape[0]
    stride = 1
    while stride < length:
        paired = vector.reshape(-1, 2, stride)
        upper = paired[:, 0, :]
        lower = paired[:, 1, :]
        vector = jnp.stack([upper + lower, upper - lower], axis=1).reshape(length)
        stride *= 2
    return vector

def reference(inputs, cotangents, sign_flips, sample_rows, sample_columns):
    part_count = N_PARAM
    rows_block = F // part_count
    owner_block = (sample_rows // rows_block).astype(jnp.int32)
    offsets = (sample_rows % rows_block * D + sample_columns).astype(jnp.int32)
    weight_table = hadamard_table(part_count)[owner_block]
    norm_factor = 1.0 / math.sqrt(F * D)

    def one_example(pair):
        activations, output_grad = pair

        def one_block(block_index):
            grad_rows = lax.dynamic_slice_in_dim(output_grad, block_index * rows_block, rows_block, 1)
            gradient = jnp.dot(grad_rows.T, activations, preferred_element_type=jnp.float32)
            flip_rows = lax.dynamic_slice_in_dim(sign_flips, block_index * rows_block, rows_block, 0)
            flipped = (gradient * flip_rows.astype(jnp.float32)).reshape(rows_block * D)
            return walsh_transform(flipped)[offsets]
        picked = lax.map(one_block, jnp.arange(part_count, dtype=jnp.int32))
        return lax.optimization_barrier(jnp.sum(picked.T * weight_table, axis=1)) * norm_factor
    return lax.map(one_example, (inputs, cotangents))
```

```python
import functools, math
import jax, jax.numpy as jnp
from jax import lax
from jax.sharding import PartitionSpec as P
from jax.experimental import pallas as pl
from jax.experimental.pallas import tpu as pltpu

def hadamard_table(order):
    p = lax.iota(jnp.int32, order)
    odd = lax.population_count(p[:, None] & p[None, :]) & 1
    return (1 - 2 * odd).astype(jnp.bfloat16)

def split(v):
    hi = v.astype(jnp.bfloat16)
    return hi, (v - hi.astype(jnp.float32)).astype(jnp.bfloat16)

def butterfly(parts):
    n = len(parts); s = 1
    parts = list(parts)
    while s < n:
        for i in range(n):
            if not i & s:
                a, b = parts[i], parts[i | s]
                parts[i], parts[i | s] = a + b, a - b
        s *= 2
    return parts

def kernel(norm, idx_ref, ct_ref, x_ref, s_ref, mt_ref, hr_ref, out_ref, t_ref, a0_ref, a1_ref):
    R, D = s_ref.shape
    L = 128
    CH = 8 * L
    nch = D // CH
    @pl.loop(0, nch)
    def _(c):
        cols = pl.ds(pl.multiple_of(c * CH, CH), CH)
        g = jnp.dot(ct_ref[...], x_ref[:, cols], preferred_element_type=jnp.float32)
        f = g * s_ref[:, cols].astype(jnp.float32)
        hi, lo = split(f)
        r = jnp.dot(hr_ref[...], jnp.concatenate([hi, lo], 0), preferred_element_type=jnp.float32)
        for t in range(R // 8):
            parts = butterfly([r[8*t:8*t+8, L*u:L*u+L] for u in range(8)])
            for u in range(8):
                t_ref[pl.ds(pl.multiple_of((c * 8 + u) * R + 8 * t, 8), 8), :] = parts[u]
    @pl.loop(0, R // 8)
    def _(t):
        for u in range(8):
            rows = [pl.ds(pl.multiple_of((8 * c + u) * R + 8 * t, 8), 8) for c in range(nch)]
            parts = butterfly([t_ref[w, :] for w in rows])
            for w, v in zip(rows, parts):
                t_ref[w, :] = v
    eye = lax.broadcasted_iota(jnp.int32, (L, L), 0) == lax.broadcasted_iota(jnp.int32, (L, L), 1)
    def gather(b, a_ref):
        for s in range(L):
            a_ref[pl.ds(s, 1), :] = t_ref[pl.ds(idx_ref[b * L + s], 1), :]
    def select(b, a_ref):
        hi, lo = split(a_ref[...])
        m = mt_ref[b]
        z = jnp.dot(jnp.concatenate([hi, lo], 1), jnp.concatenate([m, m], 0), preferred_element_type=jnp.float32)
        out_ref[pl.ds(b, 1), :] = jnp.sum(jnp.where(eye, z, 0.0), axis=0, keepdims=True) * norm
    nb = out_ref.shape[0]
    gather(0, a0_ref)
    @pl.loop(0, nb // 2)
    def _(i):
        b = 2 * i
        gather(b + 1, a1_ref)
        select(b, a0_ref)
        gather(jnp.minimum(b + 2, nb - 1), a0_ref)
        select(b + 1, a1_ref)

def local_call(idx, ct, x, s, mt, norm):
    R, D = s.shape
    n = idx.shape[0]
    h = hadamard_table(R)
    hr = jnp.concatenate([h, h], 1)
    vm = pl.BlockSpec(memory_space=pltpu.VMEM)
    return pl.pallas_call(
        functools.partial(kernel, norm),
        out_shape=jax.ShapeDtypeStruct((n // 128, 128), jnp.float32),
        in_specs=[pl.BlockSpec(memory_space=pltpu.SMEM)] + [vm] * 5,
        out_specs=vm,
        scratch_shapes=[pltpu.VMEM((R * D // 128, 128), jnp.float32), pltpu.VMEM((128, 128), jnp.float32), pltpu.VMEM((128, 128), jnp.float32)],
        compiler_params=pltpu.CompilerParams(vmem_limit_bytes=48 << 20),
    )(idx, ct, x, s, mt, hr)

def tables(rows, cols, R, p):
    idx = (cols // 128) * R + rows % R
    lane = cols % 128
    n = rows.shape[0]
    par = lax.population_count(rows // R & p) & 1
    l = lax.iota(jnp.int32, 128)
    odd = (lax.population_count(l[None, :, None] & lane.reshape(-1, 1, 128)) + par.reshape(-1, 1, 128)) & 1
    return idx, (1 - 2 * odd).astype(jnp.bfloat16)


def shards(inputs, cotangents, sign_flips, sample_rows, sample_columns):
    own = lax.axis_index("param")
    parts = lax.axis_size("param")
    zs, xs = 8, 2
    ys = parts // (zs * xs)
    device = lambda y, x, z: (y * xs + x) * zs + z
    every = [(y, x, z) for y in range(ys) for x in range(xs) for z in range(zs)]
    across = [(device(y, x, z), device(y, 1 - x, z)) for y, x, z in every]
    planes = [[device(y, x, z) for y in range(ys) for z in range(zs)] for x in range(xs)]
    rows_here, width = sign_flips.shape
    norm = 1.0 / math.sqrt(parts * rows_here * width)
    tokens = inputs[0]
    other = lax.ppermute(tokens, "param", across)
    gathered = lax.all_gather(
        jnp.concatenate([tokens, other], 0), "param", axis=0, tiled=True, axis_index_groups=planes
    )
    mine = own // zs % xs
    grad = cotangents[0].reshape(ys, xs, zs, -1, rows_here)
    grad = jnp.where(mine == 0, grad, grad[:, ::-1]).transpose(0, 2, 1, 3, 4).reshape(-1, rows_here)
    index, table = tables(sample_rows, sample_columns, rows_here, own)
    picked = local_call(index, grad.T, gathered, sign_flips, table, norm)
    pair = picked.reshape(parts, 1, -1)
    return lax.all_to_all(pair, "param", 0, 0, tiled=True).sum(0)


def solution(mesh):
    return jax.shard_map(
        shards,
        mesh=mesh,
        in_specs=(P("ex", "param", None), P("ex", None, "param"), P("param", None), P(), P()),
        out_specs=P("ex", "param"),
        check_vma=False,
    )
```

```python
import functools, math
import jax, jax.numpy as jnp
from jax import lax
from jax.sharding import PartitionSpec as P
from jax.experimental import pallas as pl
from jax.experimental.pallas import tpu as pltpu

LANES = 128
STEP = 8 * LANES


def hadamard_table(order):
    p = lax.iota(jnp.int32, order)
    odd = lax.population_count(p[:, None] & p[None, :]) & 1
    return (1 - 2 * odd).astype(jnp.bfloat16)


def split(v):
    hi = v.astype(jnp.bfloat16)
    return hi, (v - hi.astype(jnp.float32)).astype(jnp.bfloat16)


def butterfly(parts):
    parts, stride = list(parts), 1
    while stride < len(parts):
        for i in range(len(parts)):
            if not i & stride:
                a, b = parts[i], parts[i | stride]
                parts[i], parts[i | stride] = a + b, a - b
        stride *= 2
    return parts


def kernel(norm, index, core, grads, tokens, own, near, far, near_half, far_half, table, rows_sign, out, block, even, odd):
    rows = grads.shape[1]
    me = core[0]

    def chunk(signs, start, slot, half):
        cols = pl.ds(pl.multiple_of(half * STEP, STEP), STEP)
        g = jnp.dot(grads[slot], tokens[:, cols], preferred_element_type=jnp.float32)
        f = g * signs[:, pl.ds(pl.multiple_of(start, STEP), STEP)].astype(jnp.float32)
        r = jnp.dot(rows_sign[...], jnp.concatenate(split(f), 0), preferred_element_type=jnp.float32)
        for t in range(rows // 8):
            parts = butterfly([r[8 * t : 8 * t + 8, LANES * u : LANES * u + LANES] for u in range(8)])
            for u in range(8):
                base = ((slot * 2 + half) * 8 + u) * rows + 8 * t
                block[pl.ds(pl.multiple_of(base, 8), 8), :] = parts[u]

    for signs, slot in ((own, 0), (near, 2 - me), (far, 1 + me)):
        @pl.loop(0, 2)
        def _(half):
            chunk(signs, half * STEP, slot, half)
    chunk(near_half, 0, 3, me)
    chunk(far_half, 0, 3, 1 - me)

    @pl.loop(0, rows // 8)
    def _(t):
        for u in range(8):
            at = [pl.ds(pl.multiple_of((8 * c + u) * rows + 8 * t, 8), 8) for c in range(8)]
            for w, v in zip(at, butterfly([block[w, :] for w in at])):
                block[w, :] = v

    shape = (LANES, LANES)
    eye = lax.broadcasted_iota(jnp.int32, shape, 0) == lax.broadcasted_iota(jnp.int32, shape, 1)

    def gather(b, picked):
        for s in range(LANES):
            picked[pl.ds(s, 1), :] = block[pl.ds(index[b * LANES + s], 1), :]

    def select(b, picked):
        m = table[b]
        z = jnp.dot(
            jnp.concatenate(split(picked[...]), 1), jnp.concatenate([m, m], 0), preferred_element_type=jnp.float32
        )
        out[pl.ds(b, 1), :] = jnp.sum(jnp.where(eye, z, 0.0), axis=0, keepdims=True) * norm

    count = out.shape[0]
    gather(0, even)

    @pl.loop(0, count // 2)
    def _(i):
        b = 2 * i
        gather(b + 1, odd)
        select(b, even)
        gather(jnp.minimum(b + 2, count - 1), even)
        select(b + 1, odd)


def local_call(norm, index, core, grads, tokens, own, near, far, near_half, far_half, table):
    rows = grads.shape[1]
    h = hadamard_table(rows)
    samples = index.shape[0]
    smem, vmem = pl.BlockSpec(memory_space=pltpu.SMEM), pl.BlockSpec(memory_space=pltpu.VMEM)
    return pl.pallas_call(
        functools.partial(kernel, norm),
        out_shape=jax.ShapeDtypeStruct((samples // LANES, LANES), jnp.float32),
        in_specs=[smem, smem] + [vmem] * 9,
        out_specs=vmem,
        scratch_shapes=[
            pltpu.VMEM((grads.shape[0] * rows * tokens.shape[1] // LANES, LANES), jnp.float32),
            pltpu.VMEM((LANES, LANES), jnp.float32),
            pltpu.VMEM((LANES, LANES), jnp.float32),
        ],
        compiler_params=pltpu.CompilerParams(vmem_limit_bytes=40 << 20),
    )(index, core, grads, tokens, own, near, far, near_half, far_half, table, jnp.concatenate([h, h], 1))


def odd_bits(v):
    return lax.population_count(v) & 1


def shards(inputs, cotangents, sign_flips, sample_rows, sample_columns):
    zs, xs, ys, cores = 8, 2, 8, 2
    own = lax.axis_index("param")
    ex = lax.axis_index("ex")
    core = ex % cores
    parts = lax.axis_size("param")
    examples = lax.axis_size("ex")
    rows, width = sign_flips.shape
    norm = 1.0 / math.sqrt(parts * rows * width)
    shift = (0, 1, zs, zs + 1)
    place = (own >> 3 & 1) * 2 + (own & 1)
    span = width // 4

    def columns(start_place, start, size):
        return lax.dynamic_slice_in_dim(sign_flips, start_place * span + start, size, 1)

    def send(value, slot_of_core):
        pairs = [
            (p * examples + e, (p ^ shift[slot_of_core[e % cores]]) * examples + e)
            for p in range(ys * xs * zs) for e in range(examples)
        ]
        return lax.ppermute(value, ("param", "ex"), pairs)

    swap = [(e, e ^ 1) for e in range(examples)]

    near = send(columns(place ^ (2 - core), 0, span), (2, 1))
    near_half = send(columns(place ^ 3, core * (span // 2), span // 2), (3, 3))
    tokens = inputs[0].reshape(-1, xs, 2, span).transpose(1, 2, 0, 3)
    tokens = jnp.broadcast_to(tokens[None, :, None], (ys, xs, zs // 2, 2) + tokens.shape[2:])
    tokens = lax.all_to_all(tokens.reshape(parts, -1, span), "param", 0, 0, tiled=True).reshape(-1, span)
    far = lax.ppermute(near, "ex", swap)
    far_half = lax.ppermute(near_half, "ex", swap)
    grad = cotangents[0].T
    grads = jnp.stack([grad] + [send(grad, (s, s)) for s in (1, 2, 3)])

    owner, row = sample_rows // rows, sample_rows % rows
    slot = (owner >> 3 & 1) * 2 + (owner & 1)
    index = (slot * (span // LANES) + sample_columns // LANES % (span // LANES)) * rows + row
    odd = odd_bits(owner & own) + odd_bits(sample_columns // span & place)
    lane = lax.iota(jnp.int32, LANES)
    odd = odd.reshape(-1, 1, LANES) + odd_bits(lane[None, :, None] & (sample_columns % LANES).reshape(-1, 1, LANES))
    table = (1 - 2 * (odd & 1)).astype(jnp.bfloat16)

    picked = local_call(
        norm, index, core[None], grads, tokens, columns(place, 0, span), near, far, near_half, far_half, table
    )
    return lax.all_to_all(picked.reshape(parts, 1, -1), "param", 0, 0, tiled=True).sum(0)


def solution(mesh):
    return jax.shard_map(
        shards,
        mesh=mesh,
        in_specs=(P("ex", "param", None), P("ex", None, "param"), P("param", None), P(), P()),
        out_specs=P("ex", "param"),
        check_vma=False,
    )
```

```python
import functools, math
import jax, jax.numpy as jnp
from jax import lax
from jax.sharding import PartitionSpec as P
from jax.experimental import pallas as pl
from jax.experimental.pallas import tpu as pltpu

LANES = 128
STEP = 8 * LANES


def hadamard_table(order):
    p = lax.iota(jnp.int32, order)
    odd = lax.population_count(p[:, None] & p[None, :]) & 1
    return (1 - 2 * odd).astype(jnp.bfloat16)


def split(v):
    hi = v.astype(jnp.bfloat16)
    return hi, (v - hi.astype(jnp.float32)).astype(jnp.bfloat16)


def butterfly(parts):
    parts, stride = list(parts), 1
    while stride < len(parts):
        for i in range(len(parts)):
            if not i & stride:
                a, b = parts[i], parts[i | stride]
                parts[i], parts[i | stride] = a + b, a - b
        stride *= 2
    return parts


def kernel(norm, index, core, grads, tokens, own, near, far, near_half, far_half, table, rows_sign, out, *scratch):
    block, even, odd, own_v, near_v, far_v, near_half_v, far_half_v, here, later, arrived, listed = scratch
    rows = grads.shape[1]
    me = core[0]
    span = tokens.shape[1]
    group = here.shape[0]
    groups = index.shape[0] // group
    sources = (own.at[:, pl.ds(pl.multiple_of(core[1] * span, span), span)], near, far, near_half, far_half)
    signs = (own_v, near_v, far_v, near_half_v, far_half_v)
    copies = [pltpu.make_async_copy(a, b, arrived.at[i]) for i, (a, b) in enumerate(zip(sources, signs))]

    def fetch(i, part, places):
        start = pl.multiple_of(i * group, group)
        return pltpu.make_async_copy(index.at[pl.ds(start, group)], places, listed.at[part])

    for copy in copies:
        copy.start()
    fetch(0, 0, here).start()
    fetch(1, 1, later).start()

    def chunk(signs, start, slot, half):
        cols = pl.ds(pl.multiple_of(half * STEP, STEP), STEP)
        g = jnp.dot(grads[slot], tokens[:, cols], preferred_element_type=jnp.float32)
        f = g * signs[:, pl.ds(pl.multiple_of(start, STEP), STEP)].astype(jnp.float32)
        r = jnp.dot(rows_sign[...], jnp.concatenate(split(f), 0), preferred_element_type=jnp.float32)
        for t in range(rows // 8):
            parts = butterfly([r[8 * t : 8 * t + 8, LANES * u : LANES * u + LANES] for u in range(8)])
            for u in range(8):
                base = ((slot * 2 + half) * 8 + u) * rows + 8 * t
                block[pl.ds(pl.multiple_of(base, 8), 8), :] = parts[u]

    for i, slot in enumerate((0, 2 - me, 1 + me)):
        copies[i].wait()

        @pl.loop(0, 2)
        def _(half):
            chunk(signs[i], half * STEP, slot, half)
    for i, half in ((3, me), (4, 1 - me)):
        copies[i].wait()
        chunk(signs[i], 0, 3, half)

    @pl.loop(0, rows // 8)
    def _(t):
        for u in range(8):
            at = [pl.ds(pl.multiple_of((8 * c + u) * rows + 8 * t, 8), 8) for c in range(8)]
            for w, v in zip(at, butterfly([block[w, :] for w in at])):
                block[w, :] = v

    shape = (LANES, LANES)
    eye = lax.broadcasted_iota(jnp.int32, shape, 0) == lax.broadcasted_iota(jnp.int32, shape, 1)

    def gather(places, row, picked):
        for s in range(LANES):
            picked[pl.ds(s, 1), :] = block[pl.ds(places[row, s], 1), :]

    def select(b, picked):
        m = table[b]
        z = jnp.dot(
            jnp.concatenate(split(picked[...]), 1), jnp.concatenate([m, m], 0), preferred_element_type=jnp.float32
        )
        out[pl.ds(b, 1), :] = jnp.sum(jnp.where(eye, z, 0.0), axis=0, keepdims=True) * norm

    buffers = (even, odd)

    @pl.loop(0, groups // 2)
    def _(i):
        for part, places in enumerate((here, later)):
            g = 2 * i + part
            fetch(g, part, places).wait()
            for row in range(group):
                gather(places, row, buffers[row % 2])
                if row:
                    select(g * group + row - 1, buffers[1 - row % 2])

            @pl.when(i < groups // 2 - 1)
            def _():
                fetch(g + 2, part, places).start()

            select(g * group + group - 1, buffers[1 - group % 2])


def local_call(norm, index, core, grads, tokens, own, near, far, near_half, far_half, table):
    rows = grads.shape[1]
    h = hadamard_table(rows)
    smem, vmem, held = (pl.BlockSpec(memory_space=m) for m in (pltpu.SMEM, pltpu.VMEM, pl.ANY))
    places = pltpu.SMEM((8, LANES), jnp.int32)
    signs = (own, near, far, near_half, far_half)
    widths = (near.shape[1],) * 3 + (near_half.shape[1],) * 2
    return pl.pallas_call(
        functools.partial(kernel, norm),
        out_shape=jax.ShapeDtypeStruct(index.shape, jnp.float32),
        in_specs=[vmem, smem, vmem, vmem] + [held] * 5 + [vmem, vmem],
        out_specs=vmem,
        scratch_shapes=[
            pltpu.VMEM((grads.shape[0] * rows * tokens.shape[1] // LANES, LANES), jnp.float32),
            pltpu.VMEM((LANES, LANES), jnp.float32),
            pltpu.VMEM((LANES, LANES), jnp.float32),
            *(pltpu.VMEM((rows, w), own.dtype) for w in widths),
            places,
            places,
            pltpu.SemaphoreType.DMA((len(signs),)),
            pltpu.SemaphoreType.DMA((2,)),
        ],
        compiler_params=pltpu.CompilerParams(vmem_limit_bytes=40 << 20),
    )(index, core, grads, tokens, *signs, table, jnp.concatenate([h, h], 1))


def odd_bits(v):
    return lax.population_count(v) & 1


def shards(inputs, cotangents, sign_flips, sample_rows, sample_columns):
    zs, xs, ys, cores = 8, 2, 8, 2
    own = lax.axis_index("param")
    ex = lax.axis_index("ex")
    core = ex % cores
    parts = lax.axis_size("param")
    examples = lax.axis_size("ex")
    rows, width = sign_flips.shape
    norm = 1.0 / math.sqrt(parts * rows * width)
    shift = (0, 1, zs, zs + 1)
    place = (own >> 3 & 1) * 2 + (own & 1)
    span = width // 4

    def columns(start_place, start, size):
        return lax.dynamic_slice_in_dim(sign_flips, start_place * span + start, size, 1)

    def send(value, slot_of_core):
        pairs = [
            (p * examples + e, (p ^ shift[slot_of_core[e % cores]]) * examples + e)
            for p in range(ys * xs * zs) for e in range(examples)
        ]
        return lax.ppermute(value, ("param", "ex"), pairs)

    swap = [(e, e ^ 1) for e in range(examples)]

    near = send(columns(place ^ (2 - core), 0, span), (2, 1))
    near_half = send(columns(place ^ 3, core * (span // 2), span // 2), (3, 3))
    tokens = inputs[0].reshape(-1, xs, 2, span).transpose(1, 2, 0, 3)
    tokens = jnp.broadcast_to(tokens[None, :, None], (ys, xs, zs // 2, 2) + tokens.shape[2:])
    tokens = lax.all_to_all(tokens.reshape(parts, -1, span), "param", 0, 0, tiled=True)
    tokens = tokens.reshape(-1, span)
    far = lax.ppermute(near, "ex", swap)
    far_half = lax.ppermute(near_half, "ex", swap)
    grad = cotangents[0].T
    grads = [grad]
    for s in (1, 2, 3):
        grads.append(send(grad, (s, s)))
    grads = jnp.stack(grads)

    owner, row = sample_rows // rows, sample_rows % rows
    slot = (owner >> 3 & 1) * 2 + (owner & 1)
    index = (slot * (span // LANES) + sample_columns // LANES % (span // LANES)) * rows + row
    index = index.reshape(-1, LANES)
    odd = odd_bits(owner & own) + odd_bits(sample_columns // span & place)
    lane = lax.iota(jnp.int32, LANES)
    odd = odd.reshape(-1, 1, LANES) + odd_bits(lane[None, :, None] & (sample_columns % LANES).reshape(-1, 1, LANES))
    table = (1 - 2 * (odd & 1)).astype(jnp.bfloat16)

    picked = local_call(
        norm, index, jnp.stack([core, place]), grads, tokens, sign_flips, near, far, near_half, far_half, table
    )
    return lax.all_to_all(picked.reshape(parts, 1, -1), "param", 0, 0, tiled=True).sum(0)


def solution(mesh):
    return jax.shard_map(
        shards,
        mesh=mesh,
        in_specs=(P("ex", "param", None), P("ex", None, "param"), P("param", None), P(), P()),
        out_specs=P("ex", "param"),
        check_vma=False,
    )
```

```python
import functools, math
import jax, jax.numpy as jnp
from jax import lax
from jax.sharding import PartitionSpec as P
from jax.experimental import pallas as pl
from jax.experimental.pallas import tpu as pltpu

LANES = 128
STEP = 8 * LANES


def hadamard_table(order):
    p = lax.iota(jnp.int32, order)
    odd = lax.population_count(p[:, None] & p[None, :]) & 1
    return (1 - 2 * odd).astype(jnp.bfloat16)


def split(v):
    hi = v.astype(jnp.bfloat16)
    return hi, (v - hi.astype(jnp.float32)).astype(jnp.bfloat16)


def butterfly(parts):
    parts, stride = list(parts), 1
    while stride < len(parts):
        for i in range(len(parts)):
            if not i & stride:
                a, b = parts[i], parts[i | stride]
                parts[i], parts[i | stride] = a + b, a - b
        stride *= 2
    return parts


def kernel(norm, index, core, grads, tokens, own, z_mine, z_other, x_mine, x_other, table, rows_sign, out, *scratch):
    block, even, odd, signs, picks, here, later, arrived, listed = scratch
    rows = grads.shape[1]
    me = core[0]
    span = tokens.shape[1]
    group = here.shape[0]
    groups = index.shape[0] // group

    def load(source, place):
        return pltpu.make_async_copy(source, signs.at[place], arrived.at[place])

    columns = pl.ds(pl.multiple_of(core[1] * span, span), span)
    copies = (load(own.at[:, columns], 0), load(z_mine, 1), load(x_mine, 2), load(x_other, 3))

    def fetch(i, part, places):
        start = pl.multiple_of(i * group, group)
        return pltpu.make_async_copy(index.at[pl.ds(start, group)], places, listed.at[part])

    for i in (0, 2, 3):
        copies[i].start()

    @pl.when(me == 0)
    def _():
        copies[1].start()

    @pl.when(me != 0)
    def _():
        load(z_other, 1).start()

    picking = pltpu.make_async_copy(table, picks, listed.at[2])
    picking.start()
    fetch(0, 0, here).start()
    fetch(1, 1, later).start()

    def chunk(place, slot, half):
        cols = pl.ds(pl.multiple_of(half * STEP, STEP), STEP)
        g = jnp.dot(grads[slot], tokens[:, cols], preferred_element_type=jnp.float32)
        f = g * signs[place, :, cols].astype(jnp.float32)
        r = jnp.dot(rows_sign[...], jnp.concatenate(split(f), 0), preferred_element_type=jnp.float32)
        for t in range(rows // 8):
            parts = butterfly([r[8 * t : 8 * t + 8, LANES * u : LANES * u + LANES] for u in range(8)])
            for u in range(8):
                base = ((slot * 2 + half) * 8 + u) * rows + 8 * t
                block[pl.ds(pl.multiple_of(base, 8), 8), :] = parts[u]

    for i, slot in enumerate((0, 1, 2 + me, 3 - me)):
        copies[i].wait()

        @pl.loop(0, 2)
        def _(half):
            chunk(i, slot, half)

    @pl.loop(0, rows // 8)
    def _(t):
        for u in range(8):
            at = [pl.ds(pl.multiple_of((8 * c + u) * rows + 8 * t, 8), 8) for c in range(8)]
            for w, v in zip(at, butterfly([block[w, :] for w in at])):
                block[w, :] = v

    shape = (LANES, LANES)
    eye = lax.broadcasted_iota(jnp.int32, shape, 0) == lax.broadcasted_iota(jnp.int32, shape, 1)

    def gather(places, row, picked):
        for s in range(LANES):
            picked[pl.ds(s, 1), :] = block[pl.ds(places[row, s], 1), :]

    def select(b, picked):
        m = picks[b]
        z = jnp.dot(
            jnp.concatenate(split(picked[...]), 1), jnp.concatenate([m, m], 0), preferred_element_type=jnp.float32
        )
        out[pl.ds(b, 1), :] = jnp.sum(jnp.where(eye, z, 0.0), axis=0, keepdims=True) * norm

    buffers = (even, odd)
    picking.wait()

    @pl.loop(0, groups // 2)
    def _(i):
        for part, places in enumerate((here, later)):
            g = 2 * i + part
            fetch(g, part, places).wait()
            for row in range(group):
                gather(places, row, buffers[row % 2])
                if row:
                    select(g * group + row - 1, buffers[1 - row % 2])

            @pl.when(i < groups // 2 - 1)
            def _():
                fetch(g + 2, part, places).start()

            select(g * group + group - 1, buffers[1 - group % 2])


def local_call(norm, index, core, grads, tokens, signs, table):
    rows = grads.shape[1]
    h = hadamard_table(rows)
    smem, vmem, held = (pl.BlockSpec(memory_space=m) for m in (pltpu.SMEM, pltpu.VMEM, pltpu.HBM))
    places = pltpu.SMEM((8, LANES), jnp.int32)
    return pl.pallas_call(
        functools.partial(kernel, norm),
        out_shape=jax.ShapeDtypeStruct(index.shape, jnp.float32),
        in_specs=[vmem, smem, vmem, vmem] + [held] * 6 + [vmem],
        out_specs=vmem,
        scratch_shapes=[
            pltpu.VMEM((grads.shape[0] * rows * tokens.shape[1] // LANES, LANES), jnp.float32),
            pltpu.VMEM((LANES, LANES), jnp.float32),
            pltpu.VMEM((LANES, LANES), jnp.float32),
            pltpu.VMEM((4, rows, tokens.shape[1]), signs[0].dtype),
            pltpu.VMEM(table.shape, table.dtype),
            places,
            places,
            pltpu.SemaphoreType.DMA((4,)),
            pltpu.SemaphoreType.DMA((3,)),
        ],
        compiler_params=pltpu.CompilerParams(vmem_limit_bytes=50 << 20),
    )(index, core, grads, tokens, *signs, table, jnp.concatenate([h, h], 1))


def odd_bits(v):
    return lax.population_count(v) & 1


def shards(inputs, cotangents, sign_flips, sample_rows, sample_columns):
    zs, xs, ys, cores = 8, 2, 8, 2
    own = lax.axis_index("param")
    ex = lax.axis_index("ex")
    core = ex % cores
    parts = lax.axis_size("param")
    examples = lax.axis_size("ex")
    rows, width = sign_flips.shape
    norm = 1.0 / math.sqrt(parts * rows * width)
    shift = (0, 1, zs, zs + 1)
    place = (own >> 3 & 1) * 2 + (own & 1)
    span = width // 4

    def columns(start_place, start, size):
        return lax.dynamic_slice_in_dim(sign_flips, start_place * span + start, size, 1)

    def send(value, slot, cross=False):
        pairs = []
        for p in range(ys * xs * zs):
            for e in range(examples):
                to = e ^ cores if cross and e % cores else e
                pairs.append((p * examples + e, (p ^ shift[slot]) * examples + to))
        return lax.ppermute(value, ("param", "ex"), pairs)

    swap = [(e, e ^ 1) for e in range(examples)]

    z_mine = send(columns(place ^ (1 + 2 * core), 0, span), 1)
    x_mine = send(jnp.where(core == 0, columns(place ^ 2, 0, span), z_mine), 2, True)
    tokens = inputs[0].reshape(-1, xs, 2, span).transpose(1, 2, 0, 3)
    tokens = jnp.broadcast_to(tokens[None, :, None], (ys, xs, zs // 2, 2) + tokens.shape[2:])
    tokens = lax.all_to_all(tokens.reshape(parts, -1, span), "param", 0, 0, tiled=True)
    tokens = tokens.reshape(-1, span)
    z_other = lax.ppermute(z_mine, "ex", swap)
    x_other = lax.ppermute(x_mine, "ex", swap)
    grad = cotangents[0].T
    grads = [grad]
    for s in (1, 2, 3):
        grads.append(send(grad, s))
    grads = jnp.stack(grads)

    owner, row = sample_rows // rows, sample_rows % rows
    slot = (owner >> 3 & 1) * 2 + (owner & 1)
    index = (slot * (span // LANES) + sample_columns // LANES % (span // LANES)) * rows + row
    index = index.reshape(-1, LANES)
    odd = odd_bits(owner & own) + odd_bits(sample_columns // span & place)
    lane = lax.iota(jnp.int32, LANES)
    odd = odd.reshape(-1, 1, LANES) + odd_bits(lane[None, :, None] & (sample_columns % LANES).reshape(-1, 1, LANES))
    table = (1 - 2 * (odd & 1)).astype(jnp.bfloat16)

    picked = local_call(
        norm, index, jnp.stack([core, place]), grads, tokens, (sign_flips, z_mine, z_other, x_mine, x_other), table
    )
    return lax.all_to_all(picked.reshape(parts, 1, -1), "param", 0, 0, tiled=True).sum(0)


def solution(mesh):
    return jax.shard_map(
        shards,
        mesh=mesh,
        in_specs=(P("ex", "param", None), P("ex", None, "param"), P("param", None), P(), P()),
        out_specs=P("ex", "param"),
        check_vma=False,
    )
```

```python
import functools, math
import jax, jax.numpy as jnp
from jax import lax
from jax.sharding import PartitionSpec as P
from jax.experimental import pallas as pl
from jax.experimental.pallas import tpu as pltpu

LANES = 128
STEP = 8 * LANES
TILES = 2 * STEP // LANES
ROOM = 50 << 20


def hadamard_table(order):
    p = lax.iota(jnp.int32, order)
    odd = lax.population_count(p[:, None] & p[None, :]) & 1
    return (1 - 2 * odd).astype(jnp.bfloat16)


def split(v):
    hi = v.astype(jnp.bfloat16)
    return hi, (v - hi.astype(jnp.float32)).astype(jnp.bfloat16)


def butterfly(parts):
    parts, stride = list(parts), 1
    while stride < len(parts):
        for i in range(len(parts)):
            if not i & stride:
                a, b = parts[i], parts[i | stride]
                parts[i], parts[i | stride] = a + b, a - b
        stride *= 2
    return parts


def tiles(signs, start, places, arrived):
    return [
        pltpu.make_async_copy(
            signs.at[:, pl.ds(pl.multiple_of(start + i * LANES, LANES), LANES)], places.at[i], arrived.at[i]
        )
        for i in range(TILES)
    ]


def first_kernel(start, tokens, signs, grads, parcel, spread, staged, arrived, sent):
    loads = tiles(signs, start[0], parcel, arrived)
    loads.append(pltpu.make_async_copy(grads, parcel.at[pl.ds(TILES, 2)], arrived.at[TILES]))
    for load in loads:
        load.start()
    xs, repeats, zs, _, span = staged.shape
    for x in range(xs):
        for z in range(zs):
            part = tokens[:, (x * zs + z) * span : (x * zs + z + 1) * span]
            for i in range(repeats):
                staged[x, i, z] = part
    stores = [pltpu.make_async_copy(staged, spread.at[y], sent.at[y]) for y in range(spread.shape[0])]
    for store in stores:
        store.start()
    for copy in loads + stores:
        copy.wait()


def second_kernel(core, signs, received, grads, parcel, arrived):
    own = tiles(signs, core[1], parcel, arrived)
    relayed = [pltpu.make_async_copy(received.at[i], parcel.at[i], arrived.at[i]) for i in range(TILES)]

    @pl.when(core[0] == 0)
    def _():
        for copy in own:
            copy.start()

    @pl.when(core[0] != 0)
    def _():
        for copy in relayed:
            copy.start()

    more = [
        pltpu.make_async_copy(grads, parcel.at[pl.ds(TILES, 2)], arrived.at[TILES]),
        pltpu.make_async_copy(received.at[pl.ds(TILES, 2)], parcel.at[pl.ds(TILES + 2, 2)], arrived.at[TILES + 1]),
    ]
    for copy in more:
        copy.start()
    for copy in relayed + more:
        copy.wait()


def kernel(norm, index, core, tokens, own, own_grad, z_mine, z_other, x_mine, x_other, table, rows_sign, out, *scratch):
    block, even, odd, signs, flat, grads, picks, here, later, own_arrived, arrived, listed = scratch
    rows = own.shape[0]
    me = core[0]
    group = here.shape[0]
    groups = index.shape[0] // group
    own_tiles = tiles(own, core[1], signs.at[0], own_arrived)

    def load(source, place):
        return pltpu.make_async_copy(source.at[pl.ds(0, TILES)], signs.at[place], arrived.at[place])

    def load_grad(source, start, place):
        return pltpu.make_async_copy(source.at[pl.ds(start, 2)], flat.at[place], arrived.at[4 + place])

    grad_loads = (
        load_grad(own_grad, 0, 0),
        load_grad(z_mine, TILES, 1),
        load_grad(x_mine, TILES, 2),
        load_grad(x_mine, TILES + 2, 3),
    )
    copies = (None, load(z_mine, 1), load(x_mine, 2), load(x_other, 3))
    for copy in grad_loads + tuple(own_tiles) + copies[2:]:
        copy.start()

    @pl.when(me == 0)
    def _():
        copies[1].start()

    @pl.when(me != 0)
    def _():
        load(z_other, 1).start()

    def fetch(i, part, places):
        start = pl.multiple_of(i * group, group)
        return pltpu.make_async_copy(index.at[pl.ds(start, group)], places, listed.at[part])

    picking = pltpu.make_async_copy(table, picks, listed.at[2])
    picking.start()
    fetch(0, 0, here).start()
    fetch(1, 1, later).start()

    for place, copy in enumerate(grad_loads):
        copy.wait()
        grads[place] = flat[place].reshape(-1, rows).T

    def chunk(place, slot, half):
        cols = pl.ds(pl.multiple_of(half * STEP, STEP), STEP)
        g = jnp.dot(grads[slot], tokens[:, cols], preferred_element_type=jnp.float32)
        f = jnp.concatenate(
            [g[:, LANES * u : LANES * u + LANES] * signs[place, half * 8 + u].astype(jnp.float32) for u in range(8)], 1
        )
        r = jnp.dot(rows_sign[...], jnp.concatenate(split(f), 0), preferred_element_type=jnp.float32)
        for t in range(rows // 8):
            parts = butterfly([r[8 * t : 8 * t + 8, LANES * u : LANES * u + LANES] for u in range(8)])
            for u in range(8):
                base = ((slot * 2 + half) * 8 + u) * rows + 8 * t
                block[pl.ds(pl.multiple_of(base, 8), 8), :] = parts[u]

    for i, slot in enumerate((0, 1, 2 + me, 3 - me)):
        for copy in [copies[i]] if i else own_tiles:
            copy.wait()

        @pl.loop(0, 2)
        def _(half):
            chunk(i, slot, half)

    @pl.loop(0, rows // 8)
    def _(t):
        for u in range(8):
            at = [pl.ds(pl.multiple_of((8 * c + u) * rows + 8 * t, 8), 8) for c in range(8)]
            for w, v in zip(at, butterfly([block[w, :] for w in at])):
                block[w, :] = v

    shape = (LANES, LANES)
    eye = lax.broadcasted_iota(jnp.int32, shape, 0) == lax.broadcasted_iota(jnp.int32, shape, 1)

    def gather(places, row, picked):
        for s in range(LANES):
            picked[pl.ds(s, 1), :] = block[pl.ds(places[row, s], 1), :]

    def select(b, picked):
        m = picks[b]
        z = jnp.dot(
            jnp.concatenate(split(picked[...]), 1), jnp.concatenate([m, m], 0), preferred_element_type=jnp.float32
        )
        out[pl.ds(b, 1), :] = jnp.sum(jnp.where(eye, z, 0.0), axis=0, keepdims=True) * norm

    buffers = (even, odd)
    picking.wait()

    @pl.loop(0, groups // 2)
    def _(i):
        for part, places in enumerate((here, later)):
            g = 2 * i + part
            fetch(g, part, places).wait()
            for row in range(group):
                gather(places, row, buffers[row % 2])
                if row:
                    select(g * group + row - 1, buffers[1 - row % 2])

            @pl.when(i < groups // 2 - 1)
            def _():
                fetch(g + 2, part, places).start()

            select(g * group + group - 1, buffers[1 - group % 2])


def copies_call(body, results, where, operands, memory, scratch):
    return pl.pallas_call(
        body,
        out_shape=results,
        in_specs=[pl.BlockSpec(memory_space=m) for m in memory],
        out_specs=jax.tree.map(lambda m: pl.BlockSpec(memory_space=m), where),
        scratch_shapes=scratch,
        compiler_params=pltpu.CompilerParams(vmem_limit_bytes=54 << 20),
    )(*operands)


def local_call(norm, index, core, tokens, own, own_grad, parcels, table):
    rows = own.shape[0]
    h = hadamard_table(rows)
    smem, vmem, held = (pl.BlockSpec(memory_space=m) for m in (pltpu.SMEM, pltpu.VMEM, pltpu.HBM))
    places = pltpu.SMEM((8, LANES), jnp.int32)
    return pl.pallas_call(
        functools.partial(kernel, norm),
        out_shape=jax.ShapeDtypeStruct(index.shape, jnp.float32),
        in_specs=[vmem, smem, vmem] + [held] * 7 + [vmem],
        out_specs=vmem,
        scratch_shapes=[
            pltpu.VMEM((4 * rows * tokens.shape[1] // LANES, LANES), jnp.float32),
            pltpu.VMEM((LANES, LANES), jnp.float32),
            pltpu.VMEM((LANES, LANES), jnp.float32),
            pltpu.VMEM((4, TILES, rows, LANES), own.dtype),
            pltpu.VMEM((4,) + own_grad.shape, own_grad.dtype),
            pltpu.VMEM((4, rows, tokens.shape[0]), own_grad.dtype),
            pltpu.VMEM(table.shape, table.dtype),
            places,
            places,
            pltpu.SemaphoreType.DMA((TILES,)),
            pltpu.SemaphoreType.DMA((8,)),
            pltpu.SemaphoreType.DMA((3,)),
        ],
        compiler_params=pltpu.CompilerParams(vmem_limit_bytes=ROOM),
    )(index, core, tokens, own, own_grad, *parcels, table, jnp.concatenate([h, h], 1))


def odd_bits(v):
    return lax.population_count(v) & 1


def shards(inputs, cotangents, sign_flips, sample_rows, sample_columns):
    zs, xs, ys, cores = 8, 2, 8, 2
    own = lax.axis_index("param")
    ex = lax.axis_index("ex")
    core = ex % cores
    parts = lax.axis_size("param")
    examples = lax.axis_size("ex")
    rows, width = sign_flips.shape
    norm = 1.0 / math.sqrt(parts * rows * width)
    shift = (0, 1, zs, zs + 1)
    place = (own >> 3 & 1) * 2 + (own & 1)
    span = width // 4

    def send(value, slot):
        pairs = [
            (p * examples + e, (p ^ shift[slot]) * examples + e)
            for p in range(ys * xs * zs)
            for e in range(examples)
        ]
        return lax.ppermute(value, ("param", "ex"), pairs)

    swap = [(e, e ^ 1) for e in range(examples)]

    grad = cotangents[0].reshape(2, -1, rows)
    tile = jax.ShapeDtypeStruct((TILES + 2, rows, LANES), sign_flips.dtype)
    parcel, spread = copies_call(
        first_kernel,
        (tile, jax.ShapeDtypeStruct((ys, xs, zs // 2, 2, inputs.shape[1], span), inputs.dtype)),
        (pltpu.VMEM, pltpu.HBM),
        (((place ^ (1 + 2 * core)) * span)[None], inputs[0], sign_flips, grad),
        (pltpu.SMEM, pltpu.VMEM, pltpu.HBM, pltpu.HBM),
        [
            pltpu.VMEM((xs, zs // 2, 2, inputs.shape[1], span), inputs.dtype),
            pltpu.SemaphoreType.DMA((TILES + 1,)),
            pltpu.SemaphoreType.DMA((ys,)),
        ],
    )
    z_mine = send(parcel, 1)
    tokens = lax.all_to_all(spread.reshape(parts, -1, span), "param", 0, 0, tiled=True)
    tokens = tokens.reshape(-1, span)
    parcel = copies_call(
        second_kernel,
        jax.ShapeDtypeStruct((TILES + 4, rows, LANES), sign_flips.dtype),
        pltpu.VMEM,
        (jnp.stack([core, (place ^ 2) * span]), sign_flips, z_mine, grad),
        (pltpu.SMEM, pltpu.HBM, pltpu.HBM, pltpu.HBM),
        [pltpu.SemaphoreType.DMA((TILES + 2,))],
    )
    x_mine = send(parcel, 2)
    z_other = lax.ppermute(z_mine, "ex", swap)
    x_other = lax.ppermute(x_mine, "ex", swap)

    owner, row = sample_rows // rows, sample_rows % rows
    slot = (owner >> 3 & 1) * 2 + (owner & 1)
    index = (slot * (span // LANES) + sample_columns // LANES % (span // LANES)) * rows + row
    index = index.reshape(-1, LANES)
    odd = odd_bits(owner & own) + odd_bits(sample_columns // span & place)
    lane = lax.iota(jnp.int32, LANES)
    odd = odd.reshape(-1, 1, LANES) + odd_bits(lane[None, :, None] & (sample_columns % LANES).reshape(-1, 1, LANES))
    table = (1 - 2 * (odd & 1)).astype(jnp.bfloat16)

    parcels = (z_mine, z_other, x_mine, x_other)
    picked = local_call(norm, index, jnp.stack([core, place * span]), tokens, sign_flips, grad, parcels, table)
    return lax.all_to_all(picked.reshape(parts, 1, -1), "param", 0, 0, tiled=True).sum(0)


def solution(mesh):
    return jax.shard_map(
        shards,
        mesh=mesh,
        in_specs=(P("ex", "param", None), P("ex", None, "param"), P("param", None), P(), P()),
        out_specs=P("ex", "param"),
        check_vma=False,
    )
```

```python
import functools, math
import jax, jax.numpy as jnp
from jax import lax
from jax.sharding import PartitionSpec as P
from jax.experimental import pallas as pl
from jax.experimental.pallas import tpu as pltpu

LANES = 128
STEP = 8 * LANES


def hadamard_table(order):
    p = lax.iota(jnp.int32, order)
    odd = lax.population_count(p[:, None] & p[None, :]) & 1
    return (1 - 2 * odd).astype(jnp.bfloat16)


def split(v):
    hi = v.astype(jnp.bfloat16)
    return hi, (v - hi.astype(jnp.float32)).astype(jnp.bfloat16)


def butterfly(parts):
    parts, stride = list(parts), 1
    while stride < len(parts):
        for i in range(len(parts)):
            if not i & stride:
                a, b = parts[i], parts[i | stride]
                parts[i], parts[i | stride] = a + b, a - b
        stride *= 2
    return parts


def spread_kernel(tokens, spread, staged, sent):
    xs, repeats, zs, _, span = staged.shape
    for x in range(xs):
        for z in range(zs):
            part = tokens[:, (x * zs + z) * span : (x * zs + z + 1) * span]
            for i in range(repeats):
                staged[x, i, z] = part
    stores = [pltpu.make_async_copy(staged, spread.at[y], sent.at[y]) for y in range(spread.shape[0])]
    for store in stores:
        store.start()
    for store in stores:
        store.wait()


def spread_call(tokens, ys, xs, zs, span):
    shape = (xs, zs // 2, 2, tokens.shape[0], span)
    return pl.pallas_call(
        spread_kernel,
        out_shape=jax.ShapeDtypeStruct((ys,) + shape, tokens.dtype),
        in_specs=[pl.BlockSpec(memory_space=pltpu.VMEM)],
        out_specs=pl.BlockSpec(memory_space=pltpu.HBM),
        scratch_shapes=[pltpu.VMEM(shape, tokens.dtype), pltpu.SemaphoreType.DMA((ys,))],
        compiler_params=pltpu.CompilerParams(vmem_limit_bytes=54 << 20),
    )(tokens)


def kernel(norm, index, core, grads, tokens, own, z_mine, z_other, x_mine, x_other, table, rows_sign, out, *scratch):
    block, even, odd, signs, picks, here, later, arrived, listed = scratch
    rows = grads.shape[1]
    me = core[0]
    span = tokens.shape[1]
    group = here.shape[0]
    groups = index.shape[0] // group

    def load(source, place):
        return pltpu.make_async_copy(source, signs.at[place], arrived.at[place])

    columns = pl.ds(pl.multiple_of(core[1] * span, span), span)
    copies = (load(own.at[:, columns], 0), load(z_mine, 1), load(x_mine, 2), load(x_other, 3))

    def fetch(i, part, places):
        start = pl.multiple_of(i * group, group)
        return pltpu.make_async_copy(index.at[pl.ds(start, group)], places, listed.at[part])

    for i in (0, 2, 3):
        copies[i].start()

    @pl.when(me == 0)
    def _():
        copies[1].start()

    @pl.when(me != 0)
    def _():
        load(z_other, 1).start()

    picking = pltpu.make_async_copy(table, picks, listed.at[2])
    picking.start()
    fetch(0, 0, here).start()
    fetch(1, 1, later).start()

    def chunk(place, slot, half):
        cols = pl.ds(pl.multiple_of(half * STEP, STEP), STEP)
        g = jnp.dot(grads[slot], tokens[:, cols], preferred_element_type=jnp.float32)
        flips = signs[place, :, cols]
        f = jnp.concatenate([part * flips for part in split(g)], 0)
        r = jnp.dot(rows_sign[...], f, preferred_element_type=jnp.float32)
        for t in range(rows // 8):
            parts = butterfly([r[8 * t : 8 * t + 8, LANES * u : LANES * u + LANES] for u in range(8)])
            for u in range(8):
                base = ((slot * 2 + half) * 8 + u) * rows + 8 * t
                block[pl.ds(pl.multiple_of(base, 8), 8), :] = parts[u]

    for i, slot in enumerate((0, 1, 2 + me, 3 - me)):
        copies[i].wait()

        @pl.loop(0, 2)
        def _(half):
            chunk(i, slot, half)

    @pl.loop(0, rows // 8)
    def _(t):
        for u in range(8):
            at = [pl.ds(pl.multiple_of((8 * c + u) * rows + 8 * t, 8), 8) for c in range(8)]
            for w, v in zip(at, butterfly([block[w, :] for w in at])):
                block[w, :] = v

    shape = (LANES, LANES)
    eye = lax.broadcasted_iota(jnp.int32, shape, 0) == lax.broadcasted_iota(jnp.int32, shape, 1)

    def gather(places, row, picked):
        for s in range(LANES):
            picked[pl.ds(s, 1), :] = block[pl.ds(places[row, s], 1), :]

    def select(b, picked):
        m = picks[b]
        z = jnp.dot(
            jnp.concatenate(split(picked[...]), 1), jnp.concatenate([m, m], 0), preferred_element_type=jnp.float32
        )
        out[pl.ds(b, 1), :] = jnp.sum(jnp.where(eye, z, 0.0), axis=0, keepdims=True) * norm

    buffers = (even, odd)
    picking.wait()

    @pl.loop(0, groups // 2)
    def _(i):
        for part, places in enumerate((here, later)):
            g = 2 * i + part
            fetch(g, part, places).wait()
            for row in range(group):
                gather(places, row, buffers[row % 2])
                if row:
                    select(g * group + row - 1, buffers[1 - row % 2])

            @pl.when(i < groups // 2 - 1)
            def _():
                fetch(g + 2, part, places).start()

            select(g * group + group - 1, buffers[1 - group % 2])


def local_call(norm, index, core, grads, tokens, signs, table):
    rows = grads.shape[1]
    h = hadamard_table(rows)
    smem, vmem, held = (pl.BlockSpec(memory_space=m) for m in (pltpu.SMEM, pltpu.VMEM, pltpu.HBM))
    places = pltpu.SMEM((8, LANES), jnp.int32)
    return pl.pallas_call(
        functools.partial(kernel, norm),
        out_shape=jax.ShapeDtypeStruct(index.shape, jnp.float32),
        in_specs=[vmem, smem, vmem, vmem] + [held] * 6 + [vmem],
        out_specs=vmem,
        scratch_shapes=[
            pltpu.VMEM((grads.shape[0] * rows * tokens.shape[1] // LANES, LANES), jnp.float32),
            pltpu.VMEM((LANES, LANES), jnp.float32),
            pltpu.VMEM((LANES, LANES), jnp.float32),
            pltpu.VMEM((4, rows, tokens.shape[1]), signs[0].dtype),
            pltpu.VMEM(table.shape, table.dtype),
            places,
            places,
            pltpu.SemaphoreType.DMA((4,)),
            pltpu.SemaphoreType.DMA((3,)),
        ],
        compiler_params=pltpu.CompilerParams(vmem_limit_bytes=50 << 20),
    )(index, core, grads, tokens, *signs, table, jnp.concatenate([h, h], 1))


def odd_bits(v):
    return lax.population_count(v) & 1


def shards(inputs, cotangents, sign_flips, sample_rows, sample_columns):
    zs, xs, ys, cores = 8, 2, 8, 2
    own = lax.axis_index("param")
    ex = lax.axis_index("ex")
    core = ex % cores
    parts = lax.axis_size("param")
    examples = lax.axis_size("ex")
    rows, width = sign_flips.shape
    norm = 1.0 / math.sqrt(parts * rows * width)
    shift = (0, 1, zs, zs + 1)
    place = (own >> 3 & 1) * 2 + (own & 1)
    span = width // 4

    def columns(start_place, start, size):
        return lax.dynamic_slice_in_dim(sign_flips, start_place * span + start, size, 1)

    def send(value, slot, cross=False):
        pairs = []
        for p in range(ys * xs * zs):
            for e in range(examples):
                to = e ^ cores if cross and e % cores else e
                pairs.append((p * examples + e, (p ^ shift[slot]) * examples + to))
        return lax.ppermute(value, ("param", "ex"), pairs)

    swap = [(e, e ^ 1) for e in range(examples)]

    z_mine = send(columns(place ^ (1 + 2 * core), 0, span), 1)
    x_mine = send(jnp.where(core == 0, columns(place ^ 2, 0, span), z_mine), 2, True)
    tokens = spread_call(inputs[0], ys, xs, zs, span)
    tokens = lax.all_to_all(tokens.reshape(parts, -1, span), "param", 0, 0, tiled=True)
    tokens = tokens.reshape(-1, span)
    z_other = lax.ppermute(z_mine, "ex", swap)
    x_other = lax.ppermute(x_mine, "ex", swap)
    grad = cotangents[0].T
    grads = [grad]
    for s in (1, 2, 3):
        grads.append(send(grad, s))
    grads = jnp.stack(grads)

    owner, row = sample_rows // rows, sample_rows % rows
    slot = (owner >> 3 & 1) * 2 + (owner & 1)
    index = (slot * (span // LANES) + sample_columns // LANES % (span // LANES)) * rows + row
    index = index.reshape(-1, LANES)
    odd = odd_bits(owner & own) + odd_bits(sample_columns // span & place)
    lane = lax.iota(jnp.int32, LANES)
    odd = odd.reshape(-1, 1, LANES) + odd_bits(lane[None, :, None] & (sample_columns % LANES).reshape(-1, 1, LANES))
    table = (1 - 2 * (odd & 1)).astype(jnp.bfloat16)

    picked = local_call(
        norm, index, jnp.stack([core, place]), grads, tokens, (sign_flips, z_mine, z_other, x_mine, x_other), table
    )
    return lax.all_to_all(picked.reshape(parts, 1, -1), "param", 0, 0, tiled=True).sum(0)


def solution(mesh):
    return jax.shard_map(
        shards,
        mesh=mesh,
        in_specs=(P("ex", "param", None), P("ex", None, "param"), P("param", None), P(), P()),
        out_specs=P("ex", "param"),
        check_vma=False,
    )
```
